32 devices in a mesh: ctx: 8 (over z, x), tp: 4 (over y, core).
Axes of the slice: x: 2, y: 2, z: 4, core: 2. Of those that a mesh axis runs over, the one named last changes fastest.
Arguments:
- query_branch: bfloat16 [2048, 8192], P('ctx', 'tp'), may hold values from -6 to 6
- key_branch: bfloat16 [2048, 8192], P('ctx', 'tp'), may hold values from -6 to 6
- value_branch: bfloat16 [2048, 8192], P('ctx', 'tp'), may hold values from -6 to 6
- out_cotangent: bfloat16 [2048, 8192], P('ctx', 'tp'), may hold values from -6 to 6
- out_weight: bfloat16 [8192, 8192], P('tp', 'ctx'), may hold values from -0.09375 to 0.09375
- residues: float32 [512, 16], P('tp'), may hold values from -1.5 to 1.5
- decay_rates: float32 [512, 16], P('tp'), may hold values from 4.93164063e-05 to 0.0799
- skip_gains: float32 [8192], P('tp'), may hold values from 0.1 to 1.9
- record_lengths: int32 [24], replicated, may hold values from 1 to 512, 2048 in all
Outputs:
- block_output: bfloat16 [2048, 8192], P('ctx', 'tp')
- query_grad: bfloat16 [2048, 8192], P('ctx', 'tp')
- key_grad: bfloat16 [2048, 8192], P('ctx', 'tp')
- value_grad: bfloat16 [2048, 8192], P('ctx', 'tp')
The draws below stay inside these ranges and needn't reach their ends.
Inputs may be any that keep to these rules, and one draw needn't show every extreme that they name: record_lengths sum to 2048; the longest record has exactly 512 tokens.
All inputs are finite; a program needn't handle non-finite values.
Results may differ from the reference program's by a relative error of at most 0.006.
Values may be sent and summed in bfloat16 or wider, within the bound.
A program may use at most 128 MiB of HBM per device.

```python
import math
import jax
import jax.numpy as jnp
import numpy as np
from jax import lax

D = 8192
MODES = 16
GSIZE = 16
RECORDS = 24
SEQ = 2048
GROUPS = 512
RECORD_MAX = 512


def draw_decay_rates(key, part):
    grid_shape = (GROUPS, MODES)
    key_slow = jax.random.fold_in(key, 101)
    rate_values = jnp.exp(jax.random.uniform(key_slow, grid_shape, jnp.float32, math.log(0.3 / SEQ), math.log(0.0799)))
    return rate_values.astype(jnp.float32)


def strengthened(result, key, source, target, parts, factor):
    owner, partner = [(jnp.arange(result.shape[dim]) // (result.shape[dim] // parts)).reshape([-1 if axis == dim else 1 for axis in range(result.ndim)]) for dim in (source, target)]
    chosen = jax.random.permutation(key, parts)[partner]
    strong = (owner == chosen) | (owner == (partner + parts // 2) % parts)
    return jnp.where(strong, factor * result, result)


def block_levels(stream_key, dims, pieces, smallest, largest):
    factor_of = 1.0
    for dim, parts in pieces:
        steps = jax.random.uniform(jax.random.fold_in(jax.random.fold_in(stream_key, 6), dim), (parts,), jnp.float32, smallest / len(pieces), largest / len(pieces))
        factor_of = factor_of * jnp.repeat(jnp.exp(steps), dims[dim] // parts).reshape((-1,) + (1,) * (len(dims) - 1 - dim))
    return factor_of


def split_up(amount, total, most, skew):
    loads = [(1 << 20) // math.isqrt(standing ** skew) + 1 for standing in range(2, amount + 1)]
    spare, holding = total - most - (amount - 1), [1] * (amount - 1)
    while spare > 0:
        candidates = [i for i in range(amount - 1) if holding[i] < most]
        mass, left = sum([loads[i] for i in candidates]), spare
        for i in candidates:
            more = min(most - holding[i], max(1, left * loads[i] // mass), spare)
            holding[i] = holding[i] + more
            spare = spare - more
    return np.array([most] + holding)


def uneven_parts(stream_key, count, total, most, lean):
    if count == 2:
        one = jax.random.randint(stream_key, (), max(1, total - most), min(most, total - 1) + 1)
        return jnp.stack([one, total - one])
    lengths = jnp.asarray(split_up(count, total, most, lean), jnp.int32)
    twos = (count - 1) // 2
    source_of, receiver = lengths[1:1 + 2 * twos:2], lengths[2:2 + 2 * twos:2]
    margin = jnp.minimum(source_of - 1, most - receiver)
    shifted = jax.random.randint(jax.random.fold_in(stream_key, 1), (twos,), 0, 1 << 20) % (margin + 1)
    lengths = lengths.at[1:1 + 2 * twos:2].set(source_of - shifted).at[2:2 + 2 * twos:2].set(receiver + shifted)
    return lengths[jax.random.permutation(jax.random.fold_in(stream_key, 2), count)]


def bell_draw(rng, extent, spread, most, shards=(), held_as=jnp.bfloat16):
    array = jax.random.normal(rng, extent, jnp.float32) * spread
    if len(shards) > 0:
        array = block_levels(rng, extent, shards, -0.22, 0.18) * array
    return jnp.clip(array, min=-most, max=most).astype(held_as)


def gaussian_with(key, extent, width, reach, shards, heavy, held_as=jnp.bfloat16):
    drawn = width * jax.random.normal(key, extent, jnp.float32)
    if shards:
        drawn = drawn * block_levels(key, extent, shards, -0.22, 0.18)
    return jnp.clip(strengthened(drawn, jax.random.fold_in(key, 3), *heavy), -reach, reach).astype(held_as)


def setup_inputs(seed: int = 0) -> dict:
    streams_of = jax.random.split(jax.random.key(seed), 10)
    return {
        "query_branch": bell_draw(streams_of[0], (SEQ, D), 1.0, 6.0, ((0, 8), (1, 4))),
        "key_branch": bell_draw(streams_of[1], (SEQ, D), 1.0, 6.0, ((0, 8), (1, 4))),
        "value_branch": bell_draw(streams_of[2], (SEQ, D), 1.0, 6.0, ((0, 8), (1, 4))),
        "out_cotangent": bell_draw(streams_of[3], (SEQ, D), 1.0, 6.0, ((0, 8), (1, 4))),
        "out_weight": gaussian_with(streams_of[4], (D, D), D ** -0.5, 0.09375, ((0, 4), (1, 8)), (0, 1, 8, 2.0)),
        "residues": bell_draw(streams_of[5], (GROUPS, MODES), MODES ** -0.5, 1.5, ((0, 4),), jnp.float32),
        "decay_rates": draw_decay_rates(jax.random.fold_in(streams_of[9], 71), 0),
        "skip_gains": jnp.clip(1.0 + 0.18 * jax.random.normal(streams_of[7], (D,), jnp.float32), 0.1, 1.9),
        "record_lengths": uneven_parts(streams_of[8], RECORDS, SEQ, RECORD_MAX, 2).astype(jnp.int32),
    }


def reference(query_branch, key_branch, value_branch, out_cotangent, out_weight, residues, decay_rates, skip_gains, record_lengths):
    seq_len = query_branch.shape[0]
    offsets = jnp.cumsum(record_lengths) - record_lengths
    position = jnp.arange(seq_len, dtype=jnp.int32)
    is_start = jnp.any(position[:, None] == offsets[None, :], axis=1)
    keep = jnp.where(is_start, 0.0, 1.0).astype(jnp.float32)
    gated = (key_branch.astype(jnp.float32) * value_branch.astype(jnp.float32)).astype(jnp.bfloat16)
    decay_chan = jnp.repeat(jnp.exp(-decay_rates).T, GSIZE, axis=1)
    coeffs = residues * jnp.sqrt(1.0 - jnp.exp(-2.0 * decay_rates))
    coeff_chan = jnp.repeat(coeffs.T, GSIZE, axis=1)

    def forward_step(carried, inputs):
        gated_row, keep_row = inputs
        carried = decay_chan * keep_row * carried + gated_row[None, :]
        return (carried, lax.optimization_barrier(jnp.sum(coeff_chan * carried, axis=0)))
    unused, filt_sum = lax.scan(forward_step, jnp.zeros((MODES, D), jnp.float32), (gated.astype(jnp.float32), keep))
    filtered = lax.optimization_barrier(filt_sum.astype(jnp.bfloat16)).astype(jnp.float32)
    mixed = filtered + skip_gains[None, :] * gated.astype(jnp.float32)
    mixer_out = (query_branch.astype(jnp.float32) * mixed).astype(jnp.bfloat16)
    block_output = jnp.dot(mixer_out, out_weight, preferred_element_type=jnp.float32).astype(jnp.bfloat16)
    mixer_grad = jnp.dot(out_cotangent, out_weight.T, preferred_element_type=jnp.float32).astype(jnp.bfloat16)
    mixer_grad = lax.optimization_barrier(mixer_grad).astype(jnp.float32)
    filter_grad = (mixer_grad * query_branch.astype(jnp.float32)).astype(jnp.bfloat16)
    query_grad = (mixer_grad * mixed).astype(jnp.bfloat16)

    def adjoint_step(message, inputs):
        grad_row, keep_row = inputs
        adjoint = coeff_chan * grad_row[None, :] + message
        return (decay_chan * keep_row * adjoint, lax.optimization_barrier(jnp.sum(adjoint, axis=0)))
    unused_msg, adj_total = lax.scan(adjoint_step, jnp.zeros((MODES, D), jnp.float32), (filter_grad.astype(jnp.float32), keep), reverse=True)
    adjoint_sum = lax.optimization_barrier(adj_total.astype(jnp.bfloat16)).astype(jnp.float32)
    gated_grad = adjoint_sum + skip_gains[None, :] * filter_grad.astype(jnp.float32)
    key_grad = (gated_grad * value_branch.astype(jnp.float32)).astype(jnp.bfloat16)
    value_grad = (gated_grad * key_branch.astype(jnp.float32)).astype(jnp.bfloat16)
    return (block_output, query_grad, key_grad, value_grad)
```

```python
import functools

import jax
import jax.numpy as jnp
from jax import lax
from jax.experimental import pallas as pl
from jax.experimental.pallas import tpu as pltpu
from jax.sharding import Mesh, PartitionSpec as P

GSIZE = 16
LANES = 128
TILE_GROUPS = LANES // GSIZE
F32, BF16 = jnp.float32, jnp.bfloat16


def split(a):
    hi = a.astype(BF16)
    return hi, (a - hi.astype(F32)).astype(BF16)


def wide(block, length):
    return jnp.concatenate([block[...]] * (length // LANES), axis=1)


def positions(rows, length):
    return lax.broadcasted_iota(jnp.int32, (rows, length), 1).astype(F32)


def inflow_rows(rates, coeffs, pos, first):
    return coeffs * jnp.exp(-rates * (pos + 1.0)) * first


def outflow_rows(rates, pos, last):
    return jnp.exp(-rates * (pos.shape[1] - 1.0 - pos)) * last


def own_lanes(shape, group):
    lane = lax.broadcasted_iota(jnp.int32, shape, 1)
    return (lane >= group * GSIZE) & (lane < (group + 1) * GSIZE)


def weighted_state(rows, x, modes):
    hi, lo = split(rows)
    full = jnp.dot(hi, x, preferred_element_type=F32) + jnp.dot(lo, x, preferred_element_type=F32)
    state = jnp.zeros((modes, LANES), F32)
    for g in range(TILE_GROUPS):
        part = full[g * modes : (g + 1) * modes]
        state = jnp.where(own_lanes(part.shape, g), part, state)
    return state


def contract_first(a, b):
    return lax.dot_general(a, b, (((0,), (0,)), ((), ())), preferred_element_type=F32)


def from_state(rows, state, modes):
    blocks = [
        jnp.where(own_lanes(state.shape, g), state, 0.0) for g in range(TILE_GROUPS)
    ]
    state_rows = jnp.concatenate(blocks, axis=0)
    r_hi, r_lo = split(rows)
    s_hi, s_lo = split(state_rows)
    return contract_first(r_hi, s_hi) + contract_first(r_lo, s_hi) + contract_first(r_hi, s_lo)


def convolve(left, right, mask, x, modes):
    l_hi, l_lo = split(left)
    r_hi, r_lo = split(right)
    total = jnp.zeros(x.shape, F32)
    for g in range(TILE_GROUPS):
        rows = slice(g * modes, (g + 1) * modes)
        a = jnp.concatenate([l_hi[rows], l_lo[rows], l_hi[rows]], axis=0)
        b = jnp.concatenate([r_hi[rows], r_hi[rows], r_lo[rows]], axis=0)
        kernel = (contract_first(a, b) * mask).astype(BF16)
        part = jnp.dot(kernel, x, preferred_element_type=F32)
        total = jnp.where(own_lanes(x.shape, g), part, total)
    return total


def gated_of(key, value):
    return (key[...].astype(F32) * value[...].astype(F32)).astype(BF16)


def forward_state(modes, key, value, rates, last, out):
    length = key.shape[0]
    pos = positions(rates.shape[0], length)
    rows = outflow_rows(wide(rates, length), pos, last[...])
    out[...] = weighted_state(rows, gated_of(key, value), modes)


def forward_filter(modes, key, value, query, skip, rates, coeffs, first, mask, state, mixed, mixer):
    length = key.shape[0]
    pos = positions(rates.shape[0], length)
    r, c = wide(rates, length), wide(coeffs, length)
    x = gated_of(key, value)
    half = length / 2.0
    left = c * jnp.exp(-r * (pos - half))
    right = jnp.exp(r * (pos - half))
    total = convolve(left, right, mask[...], x, modes)
    total = total + from_state(inflow_rows(r, c, pos, first[...]), state[...], modes)
    result = total.astype(BF16).astype(F32) + skip[...] * x.astype(F32)
    mixed[...] = result
    mixer[...] = (query[...].astype(F32) * result).astype(BF16)


def adjoint_state(modes, grad, query, mixed, rates, coeffs, first, filter_grad, query_grad, out):
    length = grad.shape[0]
    pos = positions(rates.shape[0], length)
    r, c = wide(rates, length), wide(coeffs, length)
    g = grad[...].astype(F32)
    f = (g * query[...].astype(F32)).astype(BF16)
    filter_grad[...] = f
    query_grad[...] = (g * mixed[...]).astype(BF16)
    out[...] = weighted_state(inflow_rows(r, c, pos, first[...]), f, modes)


def adjoint_filter(modes, grad, key, value, skip, rates, coeffs, last, mask, state, key_grad, value_grad):
    length = grad.shape[0]
    pos = positions(rates.shape[0], length)
    r, c = wide(rates, length), wide(coeffs, length)
    f = grad[...]
    half = length / 2.0
    left = jnp.exp(r * (pos - half))
    right = c * jnp.exp(-r * (pos - half))
    total = convolve(left, right, mask[...], f, modes)
    total = total + from_state(outflow_rows(r, pos, last[...]), state[...], modes)
    result = total.astype(BF16).astype(F32) + skip[...] * f.astype(F32)
    key_grad[...] = (result * value[...].astype(F32)).astype(BF16)
    value_grad[...] = (result * key[...].astype(F32)).astype(BF16)


def tiled_call(body, modes, kinds, operands, outs, length, channels, flops):
    rows = TILE_GROUPS * modes
    specs = {
        "tok": pl.BlockSpec((length, LANES), lambda i: (0, i)),
        "par": pl.BlockSpec((rows, LANES), lambda i: (i, 0)),
        "row": pl.BlockSpec((1, length), lambda i: (0, 0)),
        "skip": pl.BlockSpec((1, LANES), lambda i: (0, i)),
        "mask": pl.BlockSpec((length, length), lambda i: (0, 0)),
        "state": pl.BlockSpec((modes, LANES), lambda i: (0, i)),
    }
    shapes = {"tok": (length, channels), "state": (modes, channels)}
    moved = sum(o.size * o.dtype.itemsize for o in operands)
    return pl.pallas_call(
        functools.partial(body, modes),
        grid=(channels // LANES,),
        in_specs=[specs[k] for k in kinds],
        out_specs=[specs[k] for k, _ in outs],
        out_shape=[jax.ShapeDtypeStruct(shapes[k], d) for k, d in outs],
        cost_estimate=pl.CostEstimate(flops=flops, bytes_accessed=moved, transcendentals=0),
    )(*operands)


def on_device(
    query_branch,
    key_branch,
    value_branch,
    out_cotangent,
    out_weight,
    residues,
    decay_rates,
    skip_gains,
    record_lengths,
):
    length, channels = query_branch.shape
    modes = residues.shape[1]
    nz, nx, ntp = lax.axis_size("z"), lax.axis_size("x"), lax.axis_size("tp")
    ctx = nz * nx
    hops = -(-(length * ctx // 4) // length)
    index = lax.axis_index("z") * nx + lax.axis_index("x")

    transposed = [
        ((z * nx + x) * ntp + t, (t * nx + x) * ntp + z)
        for z in range(nz)
        for x in range(nx)
        for t in range(ntp)
    ]
    cot = lax.ppermute(out_cotangent, ("z", "x", "tp"), transposed)
    cot_all = lax.all_gather(cot, "tp", axis=0, tiled=True)
    weight = lax.all_gather(out_weight, "x", axis=1, tiled=True)

    offsets = jnp.cumsum(record_lengths) - record_lengths
    everywhere = jnp.arange(length * ctx, dtype=jnp.int32)
    starts = jnp.any(everywhere[:, None] == offsets[None, :], axis=1).astype(jnp.int32)
    starts = starts.reshape(ctx, length)
    closed = jnp.max(starts, axis=1)
    flags = lax.dynamic_index_in_dim(starts, index, 0, keepdims=False)
    segment = jnp.cumsum(flags)
    first = (segment == 0).astype(F32)[None, :]
    last = (segment == segment[-1]).astype(F32)[None, :]
    at = jnp.arange(length)
    mask = ((at[:, None] >= at[None, :]) & (segment[:, None] == segment[None, :])).astype(F32)

    coeffs = residues * jnp.sqrt(1.0 - jnp.exp(-2.0 * decay_rates))
    rates_rows = jnp.broadcast_to(decay_rates.reshape(-1, 1), (decay_rates.size, LANES))
    coeff_rows = jnp.broadcast_to(coeffs.reshape(-1, 1), (coeffs.size, LANES))
    through = jnp.repeat(jnp.exp(-decay_rates * length).T, GSIZE, axis=1)
    skip = skip_gains[None, :]
    tiles = channels // LANES
    conv_flops = tiles * TILE_GROUPS * 2 * length * length * 512
    state_flops = tiles * 2 * 256 * 256 * length

    def gathered_state(state, direction):
        total = jnp.zeros_like(state)
        factor = jnp.ones_like(state)
        for hop in range(1, hops + 1):
            pairs = [
                (c, c + direction * hop) for c in range(ctx) if 0 <= c + direction * hop < ctx
            ]
            total = total + factor * lax.ppermute(state, ("z", "x"), pairs)
            passed = jnp.clip(index - direction * hop, 0, ctx - 1)
            open_here = 1.0 - closed[passed].astype(F32)
            factor = factor * through * open_here
        return total

    (own,) = tiled_call(
        forward_state, modes, ("tok", "tok", "par", "row"),
        (key_branch, value_branch, rates_rows, last),
        (("state", F32),), length, channels, state_flops,
    )
    entering = gathered_state(own, 1)
    mixed, mixer_out = tiled_call(
        forward_filter, modes,
        ("tok", "tok", "tok", "skip", "par", "par", "row", "mask", "state"),
        (key_branch, value_branch, query_branch, skip, rates_rows, coeff_rows, first, mask, entering),
        (("tok", F32), ("tok", BF16)), length, channels, conv_flops,
    )
    mixer_all = lax.all_gather(mixer_out, "z", axis=0, tiled=True)

    back = lax.dot_general(
        cot_all, weight, (((1,), (1,)), ((), ())), preferred_element_type=F32
    ).astype(BF16)
    mixer_grad = lax.psum_scatter(back, "z", scatter_dimension=0, tiled=True)
    partial = jnp.dot(mixer_all, weight, preferred_element_type=F32).astype(BF16)
    summed = lax.psum_scatter(partial, "tp", scatter_dimension=0, tiled=True)
    block_output = lax.ppermute(summed, ("z", "x", "tp"), transposed)

    filter_grad, query_grad, own = tiled_call(
        adjoint_state, modes, ("tok", "tok", "tok", "par", "par", "row"),
        (mixer_grad, query_branch, mixed, rates_rows, coeff_rows, first),
        (("tok", BF16), ("tok", BF16), ("state", F32)), length, channels, state_flops,
    )
    entering = gathered_state(own, -1)
    key_grad, value_grad = tiled_call(
        adjoint_filter, modes,
        ("tok", "tok", "tok", "skip", "par", "par", "row", "mask", "state"),
        (filter_grad, key_branch, value_branch, skip, rates_rows, coeff_rows, last, mask.T, entering),
        (("tok", BF16), ("tok", BF16)), length, channels, conv_flops,
    )
    return (block_output, query_grad, key_grad, value_grad)


def solution(mesh):
    ctx, tp = mesh.devices.shape
    fine = Mesh(mesh.devices.reshape(tp, ctx // tp, tp), ("z", "x", "tp"))
    tokens = P(("z", "x"), "tp")
    placed = (
        tokens,
        tokens,
        tokens,
        tokens,
        P("tp", ("z", "x")),
        P("tp", None),
        P("tp", None),
        P("tp"),
        P(),
    )
    return jax.shard_map(
        on_device,
        mesh=fine,
        in_specs=placed,
        out_specs=(tokens, tokens, tokens, tokens),
        check_vma=False,
    )
```

```python
import functools

import jax
import jax.numpy as jnp
from jax import lax
from jax.experimental import pallas as pl
from jax.experimental.pallas import tpu as pltpu
from jax.sharding import Mesh, PartitionSpec as P

GSIZE = 16
LANES = 128
TILE_GROUPS = LANES // GSIZE
F32, BF16 = jnp.float32, jnp.bfloat16


def split(a):
    hi = a.astype(BF16)
    return hi, (a - hi.astype(F32)).astype(BF16)


def wide(block, length):
    return jnp.concatenate([block[...]] * (length // LANES), axis=1)


def positions(rows, length):
    return lax.broadcasted_iota(jnp.int32, (rows, length), 1).astype(F32)


def inflow_rows(rates, coeffs, pos, first):
    return coeffs * jnp.exp(-rates * (pos + 1.0)) * first


def outflow_rows(rates, pos, last):
    return jnp.exp(-rates * (pos.shape[1] - 1.0 - pos)) * last


def own_lanes(shape, group):
    lane = lax.broadcasted_iota(jnp.int32, shape, 1)
    return (lane >= group * GSIZE) & (lane < (group + 1) * GSIZE)


def weighted_state(rows, x, modes):
    hi, lo = split(rows)
    full = jnp.dot(hi, x, preferred_element_type=F32) + jnp.dot(lo, x, preferred_element_type=F32)
    state = jnp.zeros((modes, LANES), F32)
    for g in range(TILE_GROUPS):
        part = full[g * modes : (g + 1) * modes]
        state = jnp.where(own_lanes(part.shape, g), part, state)
    return state


def contract_first(a, b):
    return lax.dot_general(a, b, (((0,), (0,)), ((), ())), preferred_element_type=F32)


def from_state(rows, state, modes):
    blocks = [
        jnp.where(own_lanes(state.shape, g), state, 0.0) for g in range(TILE_GROUPS)
    ]
    state_rows = jnp.concatenate(blocks, axis=0)
    r_hi, r_lo = split(rows)
    s_hi, s_lo = split(state_rows)
    return contract_first(r_hi, s_hi) + contract_first(r_lo, s_hi) + contract_first(r_hi, s_lo)


def convolve(left, right, mask, x, modes):
    l_hi, l_lo = split(left)
    r_hi, r_lo = split(right)
    total = jnp.zeros(x.shape, F32)
    for g in range(TILE_GROUPS):
        rows = slice(g * modes, (g + 1) * modes)
        a = jnp.concatenate([l_hi[rows], l_lo[rows], l_hi[rows]], axis=0)
        b = jnp.concatenate([r_hi[rows], r_hi[rows], r_lo[rows]], axis=0)
        kernel = (contract_first(a, b) * mask).astype(BF16)
        part = jnp.dot(kernel, x, preferred_element_type=F32)
        total = jnp.where(own_lanes(x.shape, g), part, total)
    return total


def gated_of(key, value):
    return (key[...].astype(F32) * value[...].astype(F32)).astype(BF16)


def forward_state(modes, key, value, rates, last, out):
    length = key.shape[0]
    pos = positions(rates.shape[0], length)
    rows = outflow_rows(wide(rates, length), pos, last[...])
    out[...] = weighted_state(rows, gated_of(key, value), modes)


def forward_filter(modes, key, value, query, skip, rates, coeffs, first, mask, state, mixed, mixer):
    length = key.shape[0]
    pos = positions(rates.shape[0], length)
    r, c = wide(rates, length), wide(coeffs, length)
    x = gated_of(key, value)
    half = length / 2.0
    left = c * jnp.exp(-r * (pos - half))
    right = jnp.exp(r * (pos - half))
    total = convolve(left, right, mask[...], x, modes)
    total = total + from_state(inflow_rows(r, c, pos, first[...]), state[...], modes)
    result = total.astype(BF16).astype(F32) + skip[...] * x.astype(F32)
    mixed[...] = result
    mixer[...] = (query[...].astype(F32) * result).astype(BF16)


def adjoint_state(modes, grad, query, mixed, rates, coeffs, first, filter_grad, query_grad, out):
    length = grad.shape[0]
    pos = positions(rates.shape[0], length)
    r, c = wide(rates, length), wide(coeffs, length)
    g = grad[...].astype(F32)
    f = (g * query[...].astype(F32)).astype(BF16)
    filter_grad[...] = f
    query_grad[...] = (g * mixed[...]).astype(BF16)
    out[...] = weighted_state(inflow_rows(r, c, pos, first[...]), f, modes)


def adjoint_filter(modes, grad, key, value, skip, rates, coeffs, last, mask, state, key_grad, value_grad):
    length = grad.shape[0]
    pos = positions(rates.shape[0], length)
    r, c = wide(rates, length), wide(coeffs, length)
    f = grad[...]
    half = length / 2.0
    left = jnp.exp(r * (pos - half))
    right = c * jnp.exp(-r * (pos - half))
    total = convolve(left, right, mask[...], f, modes)
    total = total + from_state(outflow_rows(r, pos, last[...]), state[...], modes)
    result = total.astype(BF16).astype(F32) + skip[...] * f.astype(F32)
    key_grad[...] = (result * value[...].astype(F32)).astype(BF16)
    value_grad[...] = (result * key[...].astype(F32)).astype(BF16)


def tiled_call(body, modes, kinds, operands, outs, length, channels, flops):
    rows = TILE_GROUPS * modes
    specs = {
        "tok": pl.BlockSpec((length, LANES), lambda i: (0, i)),
        "par": pl.BlockSpec((rows, LANES), lambda i: (i, 0)),
        "row": pl.BlockSpec((1, length), lambda i: (0, 0)),
        "skip": pl.BlockSpec((1, LANES), lambda i: (0, i)),
        "mask": pl.BlockSpec((length, length), lambda i: (0, 0)),
        "state": pl.BlockSpec((modes, LANES), lambda i: (0, i)),
    }
    shapes = {"tok": (length, channels), "state": (modes, channels)}
    moved = sum(o.size * o.dtype.itemsize for o in operands)
    return pl.pallas_call(
        functools.partial(body, modes),
        grid=(channels // LANES,),
        in_specs=[specs[k] for k in kinds],
        out_specs=[specs[k] for k, _ in outs],
        out_shape=[jax.ShapeDtypeStruct(shapes[k], d) for k, d in outs],
        cost_estimate=pl.CostEstimate(flops=flops, bytes_accessed=moved, transcendentals=0),
    )(*operands)


def on_device(
    query_branch,
    key_branch,
    value_branch,
    out_cotangent,
    out_weight,
    residues,
    decay_rates,
    skip_gains,
    record_lengths,
):
    length, channels = query_branch.shape
    modes = residues.shape[1]
    nz, nx, ntp = lax.axis_size("z"), lax.axis_size("x"), lax.axis_size("tp")
    ctx = nz * nx
    hops = -(-(length * ctx // 4) // length)
    index = lax.axis_index("z") * nx + lax.axis_index("x")

    transposed = [
        ((z * nx + x) * ntp + t, (t * nx + x) * ntp + z)
        for z in range(nz)
        for x in range(nx)
        for t in range(ntp)
    ]
    cot = lax.ppermute(out_cotangent, ("z", "x", "tp"), transposed)
    cot_all = lax.all_gather(cot, "tp", axis=0, tiled=True)
    depth, width = out_weight.shape
    weight = jnp.zeros((depth, nx * width), out_weight.dtype)
    for shift in range(nx):
        block = out_weight
        if shift:
            block = lax.ppermute(out_weight, "x", [(x, (x + shift) % nx) for x in range(nx)])
        owner = lax.rem(lax.axis_index("x") - shift + nx, nx)
        weight = lax.dynamic_update_slice_in_dim(weight, block, owner * width, 1)

    offsets = jnp.cumsum(record_lengths) - record_lengths
    everywhere = jnp.arange(length * ctx, dtype=jnp.int32)
    starts = jnp.any(everywhere[:, None] == offsets[None, :], axis=1).astype(jnp.int32)
    starts = starts.reshape(ctx, length)
    closed = jnp.max(starts, axis=1)
    flags = lax.dynamic_index_in_dim(starts, index, 0, keepdims=False)
    segment = jnp.cumsum(flags)
    first = (segment == 0).astype(F32)[None, :]
    last = (segment == segment[-1]).astype(F32)[None, :]
    at = jnp.arange(length)
    mask = ((at[:, None] >= at[None, :]) & (segment[:, None] == segment[None, :])).astype(F32)

    coeffs = residues * jnp.sqrt(1.0 - jnp.exp(-2.0 * decay_rates))
    rates_rows = jnp.broadcast_to(decay_rates.reshape(-1, 1), (decay_rates.size, LANES))
    coeff_rows = jnp.broadcast_to(coeffs.reshape(-1, 1), (coeffs.size, LANES))
    through = jnp.repeat(jnp.exp(-decay_rates * length).T, GSIZE, axis=1)
    skip = skip_gains[None, :]
    tiles = channels // LANES
    conv_flops = tiles * TILE_GROUPS * 2 * length * length * 512
    state_flops = tiles * 2 * 256 * 256 * length

    def gathered_state(state, direction):
        total = jnp.zeros_like(state)
        factor = jnp.ones_like(state)
        for hop in range(1, hops + 1):
            pairs = [
                (c, c + direction * hop) for c in range(ctx) if 0 <= c + direction * hop < ctx
            ]
            total = total + factor * lax.ppermute(state, ("z", "x"), pairs)
            passed = jnp.clip(index - direction * hop, 0, ctx - 1)
            open_here = 1.0 - closed[passed].astype(F32)
            factor = factor * through * open_here
        return total

    (own,) = tiled_call(
        forward_state, modes, ("tok", "tok", "par", "row"),
        (key_branch, value_branch, rates_rows, last),
        (("state", F32),), length, channels, state_flops,
    )
    entering = gathered_state(own, 1)
    mixed, mixer_out = tiled_call(
        forward_filter, modes,
        ("tok", "tok", "tok", "skip", "par", "par", "row", "mask", "state"),
        (key_branch, value_branch, query_branch, skip, rates_rows, coeff_rows, first, mask, entering),
        (("tok", F32), ("tok", BF16)), length, channels, conv_flops,
    )
    mixer_all = lax.all_gather(mixer_out, "z", axis=0, tiled=True)

    back = lax.dot_general(
        cot_all, weight, (((1,), (1,)), ((), ())), preferred_element_type=F32
    ).astype(BF16)
    mixer_grad = lax.psum_scatter(back, "z", scatter_dimension=0, tiled=True)
    partial = jnp.dot(mixer_all, weight, preferred_element_type=F32).astype(BF16)
    summed = lax.psum_scatter(partial, "tp", scatter_dimension=0, tiled=True)
    block_output = lax.ppermute(summed, ("z", "x", "tp"), transposed)

    filter_grad, query_grad, own = tiled_call(
        adjoint_state, modes, ("tok", "tok", "tok", "par", "par", "row"),
        (mixer_grad, query_branch, mixed, rates_rows, coeff_rows, first),
        (("tok", BF16), ("tok", BF16), ("state", F32)), length, channels, state_flops,
    )
    entering = gathered_state(own, -1)
    key_grad, value_grad = tiled_call(
        adjoint_filter, modes,
        ("tok", "tok", "tok", "skip", "par", "par", "row", "mask", "state"),
        (filter_grad, key_branch, value_branch, skip, rates_rows, coeff_rows, last, mask.T, entering),
        (("tok", BF16), ("tok", BF16)), length, channels, conv_flops,
    )
    return (block_output, query_grad, key_grad, value_grad)


def solution(mesh):
    ctx, tp = mesh.devices.shape
    fine = Mesh(mesh.devices.reshape(tp, ctx // tp, tp), ("z", "x", "tp"))
    tokens = P(("z", "x"), "tp")
    placed = (
        tokens,
        tokens,
        tokens,
        tokens,
        P("tp", ("z", "x")),
        P("tp", None),
        P("tp", None),
        P("tp"),
        P(),
    )
    return jax.shard_map(
        on_device,
        mesh=fine,
        in_specs=placed,
        out_specs=(tokens, tokens, tokens, tokens),
        check_vma=False,
    )
```
